32 devices in a mesh: groups: 2 (over y), blk: 4 (over z), uly: 2 (over x), cfg: 2 (over core).
Axes of the slice: x: 2, y: 2, z: 4, core: 2. Of those that a mesh axis runs over, the one named last changes fastest.
Arguments:
- query_rows: bfloat16 [2, 1024, 1536], P('cfg', ('groups', 'blk', 'uly')), parts along dimension 1, may hold values from -6 to 6
- key_rows: bfloat16 [2, 1024, 1536], P('cfg', ('groups', 'blk', 'uly')), parts along dimension 1, may hold values from -6 to 6
- value_rows: bfloat16 [2, 1024, 1536], P('cfg', ('groups', 'blk', 'uly')), parts along dimension 1, may hold values from -6 to 6
Outputs:
- attended: bfloat16 [2, 1024, 1536], P('cfg', ('groups', 'blk', 'uly')), parts along dimension 1
The draws below stay inside these ranges and needn't reach their ends.
There are 2 independent parts, one for each index of `groups`. The reference program is written for one: setup_inputs(seed, part) draws one part's arguments, and reference() takes and returns one part's arrays. A program takes and returns all parts, laid end to end along the dimension named above; each array names one. Nothing has to cross between parts.
All inputs are finite; a program needn't handle non-finite values.
Results may differ from the reference program's by a relative error of at most 0.0045.
Values may be sent and summed in bfloat16 or wider, within the bound.
A program may use at most 128 MiB of HBM per device.

```python
import math
import jax
import jax.numpy as jnp
from jax import lax

HEADS = 12
HD = 128
BRANCHES = 2
WIDTH = 1536
SEQ = 512


def joint_draw(key, which_one):
    shape = (BRANCHES, SEQ, WIDTH)
    own_key = jax.random.fold_in(key, 11 + which_one)
    base = jnp.clip(1.58 * jax.random.normal(own_key, shape, jnp.float32), -6.0, 6.0)
    return base.astype(jnp.bfloat16)


def draw_query_rows(key, part):
    return joint_draw(key, 0)


def draw_key_rows(key, part):
    return joint_draw(key, 1)


def shard_levels(rng, shape, split, low, top_value):
    loudness, own = 1.0, jax.random.fold_in(rng, 6)
    for axis_at, shards_of in split:
        heights = jnp.exp(jax.random.uniform(jax.random.fold_in(own, axis_at), (shards_of,), jnp.float32, low / len(split), top_value / len(split)))
        loudness = loudness * jnp.repeat(heights, shape[axis_at] // shards_of).reshape([-1 if axis == axis_at else 1 for axis in range(len(shape))])
    return loudness


def scatter_about(rng, shape, spread, most, shards=(), kind=jnp.bfloat16):
    loudness = shard_levels(rng, shape, shards, -0.22, 0.18) if shards else 1.0
    values = jax.random.normal(rng, shape, jnp.float32) * spread * loudness
    return jnp.minimum(jnp.maximum(values, -most), most).astype(kind)


def setup_inputs(seed: int = 0, part: int = 0) -> dict:
    arg_keys = jax.random.split(jax.random.key(seed), 4)
    part_splits = jax.random.split(jax.random.fold_in(arg_keys[3], part), 4)
    return {
        "query_rows": draw_query_rows(jax.random.fold_in(jax.random.fold_in(arg_keys[3], part), 71), part),
        "key_rows": draw_key_rows(jax.random.fold_in(jax.random.fold_in(arg_keys[3], part), 71), part),
        "value_rows": scatter_about(part_splits[2], (BRANCHES, SEQ, WIDTH), 1.0, 6.0, ((0, 2), (1, 8))),
    }


def one_head(triple):
    query_head, key_head, value_head = triple
    score_scale = 1.0 / math.sqrt(HD)
    scores = jnp.dot(query_head, key_head.T, preferred_element_type=jnp.float32) * score_scale
    row_max = lax.optimization_barrier(jnp.max(scores, axis=1, keepdims=True))
    weights = jnp.exp(scores - row_max)
    totals = lax.optimization_barrier(jnp.sum(weights, axis=1, keepdims=True))
    probabilities = weights.astype(jnp.bfloat16)
    mixed = jnp.dot(probabilities, value_head, preferred_element_type=jnp.float32)
    return (mixed / totals).astype(jnp.bfloat16)

def heads_first(array):
    return array.reshape(BRANCHES, SEQ, HEADS, HD).transpose(0, 2, 1, 3).reshape(BRANCHES * HEADS, SEQ, HD)

def reference(query_rows, key_rows, value_rows):
    result = lax.map(one_head, (heads_first(query_rows), heads_first(key_rows), heads_first(value_rows)))
    return result.reshape(BRANCHES, HEADS, SEQ, HD).transpose(0, 2, 1, 3).reshape(BRANCHES, SEQ, WIDTH)
```

```python
import functools
import math

import jax
import jax.numpy as jnp
from jax import lax
from jax.experimental import pallas as pl
from jax.experimental.pallas import tpu as pltpu
from jax.sharding import PartitionSpec as P

HD = 128
MESH = pl.DeviceIdType.MESH


def attend(queries, key_part, value_part):
    query_mat = queries[0, :, 0]
    row_count, head_count, head_size = query_mat.shape
    score_scale = 1.0 / math.sqrt(head_size)
    start_state = (
        jnp.full((head_count, row_count), -1e30, jnp.float32),
        jnp.zeros((head_count, row_count), jnp.float32),
        jnp.zeros((row_count, head_count, head_size), jnp.float32),
    )

    def absorb(state, pieces):
        key_piece = pieces[0][0, :, 0]
        value_piece = pieces[1][0, :, 0]
        scores = (
            jnp.einsum("qhd,khd->hqk", query_mat, key_piece, preferred_element_type=jnp.float32)
            * score_scale
        )
        running, totals, accumulated = state
        new_max = jnp.maximum(running, jnp.max(scores, axis=2))
        weights = jnp.exp(scores - new_max[:, :, None])
        factor = jnp.exp(running - new_max)
        totals = totals * factor + jnp.sum(weights, axis=2)
        probabilities = weights.astype(jnp.bfloat16)
        contrib = jnp.einsum(
            "hqk,khd->qhd", probabilities, value_piece, preferred_element_type=jnp.float32
        )
        accumulated = accumulated * factor.T[:, :, None] + contrib
        return (new_max, totals, accumulated)

    whole_keys, whole_values = (
        lax.all_gather(key_part, "blk", axis=1, tiled=True),
        lax.all_gather(value_part, "blk", axis=1, tiled=True),
    )
    key_count = whole_keys.shape[1]
    block_rows = math.gcd(key_count, 1024)

    def one_block(state, counter):
        offset = counter * block_rows
        key_block = lax.dynamic_slice_in_dim(whole_keys, offset, block_rows, 1)
        value_block = lax.dynamic_slice_in_dim(whole_values, offset, block_rows, 1)
        return (absorb(state, (key_block, value_block)), None)

    result, unused = lax.scan(
        one_block, start_state, jnp.arange(key_count // block_rows, dtype=jnp.int32)
    )
    output = (result[2] / result[1].T[:, :, None]).astype(jnp.bfloat16)
    return output.reshape(1, row_count, 1, head_count, head_size)


def gathered(query_rows, key_rows, value_rows):
    ulysses = lax.axis_size("uly")
    tokens = query_rows.shape[1]
    width = query_rows.shape[2]
    heads_local = width // HD // ulysses

    def moved(array):
        sections = array.reshape(1, tokens, ulysses, heads_local, HD)
        return lax.all_to_all(sections, "uly", split_axis=2, concat_axis=1, tiled=True)

    mixed = attend(moved(query_rows), moved(key_rows), moved(value_rows))
    merged = lax.all_to_all(mixed, "uly", split_axis=1, concat_axis=2, tiled=True)
    return merged.reshape(1, tokens, width)


def exchange_kernel(
    blocks, ulys, rows, heads, q_ref, k_ref, v_ref, o_ref,
    qb, kb, vb, ob, sb, ib, tb,
    in_send, in_recv, out_send, out_recv, row_in,
):
    half = blocks // 2
    owners = half * ulys
    slots = heads // owners
    near = owners * rows
    z = lax.axis_index("blk")
    x = lax.axis_index("uly")
    me = z * ulys + x
    side = z // half
    rank = lax.rem(me, owners)
    sources = (q_ref, k_ref, v_ref)
    buffers = (qb, kb, vb)
    fold = (1.0 / math.sqrt(HD)) * math.log2(math.e)

    def landing(t, j):
        begin = (me if t == 0 else rank) * rows
        return buffers[t].at[j, pl.ds(pl.multiple_of(begin, rows), rows)]

    def arrival(t, j, cross):
        return in_recv.at[j, 3 if cross else t]

    def piece(t, j, pz, px):
        head = (lax.rem(pz, half) * ulys + px) * slots + j
        return sources[t].at[0, :, pl.ds(pl.multiple_of(head * HD, HD), HD)]

    def send(j, pz, px, cross):
        for t in range(1 if cross else 3):
            pltpu.make_async_remote_copy(
                src_ref=piece(t, j, pz, px),
                dst_ref=landing(t, j),
                send_sem=in_send.at[j, t],
                recv_sem=arrival(t, j, cross),
                device_id={"blk": pz, "uly": px},
                device_id_type=MESH,
            ).start()

    barrier = pltpu.get_barrier_semaphore()

    def greet(pz, px):
        pl.semaphore_signal(
            barrier, inc=1, device_id={"blk": pz, "uly": px}, device_id_type=MESH
        )

    pl.when(z > 0)(lambda: greet(z - 1, x))
    pl.when(z < blocks - 1)(lambda: greet(z + 1, x))
    for d in range(1, ulys):
        greet(z, lax.rem(x + d, ulys))
    for j in range(slots):
        for t in range(3):
            pltpu.make_async_copy(
                piece(t, j, z, x), landing(t, j), arrival(t, j, False)
            ).start()
    greeted = (ulys - 1) + jnp.where(z > 0, 1, 0) + jnp.where(z < blocks - 1, 1, 0)
    pl.semaphore_wait(barrier, greeted)

    def token(row, to):
        pl.semaphore_signal(
            row_in.at[row], inc=1, device_id={"blk": to, "uly": x}, device_id_type=MESH
        )

    def send_inputs(zz):
        toward = 1 if zz < half else -1
        sent = set()

        def crosses(pz):
            return pz // half != zz // half

        def give(j, pz, e):
            if (j, pz, e) not in sent:
                sent.add((j, pz, e))
                send(j, pz, lax.rem(x + e, ulys), crosses(pz))

        def hear(pz):
            pl.semaphore_wait(row_in.at[pz], 1)
            onward = zz - 1 if pz > zz else zz + 1
            if 0 <= onward < blocks:
                token(pz, onward)

        def row(j, pz):
            for e in range(ulys):
                if pz != zz or e:
                    give(j, pz, e)

        beside = [zz + s for s in (toward, -toward) if 0 <= zz + s < blocks]
        for pz in beside:
            token(zz, pz)
        for pz in beside:
            for j in range(min(slots, 2) if crosses(pz) else 1):
                give(j, pz, 0)
        row(0, zz)
        for d in range(1, blocks):
            for s in (toward, -toward):
                pz = zz + s * d
                if 0 <= pz < blocks:
                    hear(pz)
                    row(0, pz)
        away = sorted((pz for pz in range(blocks) if crosses(pz)), key=lambda pz: abs(pz - zz))
        mine = sorted((pz for pz in range(blocks) if not crosses(pz)), key=lambda pz: -abs(pz - zz))
        for j in range(1, slots):
            if j < slots - 1:
                for pz in mine:
                    row(j, pz)
            for pz in away:
                row(j, pz)
            if j == slots - 1:
                for pz in mine:
                    row(j, pz)

    for zz in range(blocks):
        pl.when(z == zz)(functools.partial(send_inputs, zz))

    def await_bytes(ref, sem):
        pltpu.make_async_copy(ref, ref, sem).wait()

    def side_rows(which):
        return pl.ds(pl.multiple_of(which * near, near), near)

    def send_output(j, c, px):
        to = c * ulys + px
        copies = (
            (ob.at[j, pl.ds(pl.multiple_of(to * rows, rows), rows)], ib.at[side, j, rank], 0),
            (sb.at[j, to], tb.at[side, j, rank], 1),
        )
        own = to == me

        @pl.when(own)
        def _():
            for src, dst, t in copies:
                pltpu.make_async_copy(src, dst, out_recv.at[side, j, t]).start()

        @pl.when(jnp.logical_not(own))
        def _():
            for src, dst, t in copies:
                pltpu.make_async_remote_copy(
                    src_ref=src, dst_ref=dst,
                    send_sem=out_send.at[j, t], recv_sem=out_recv.at[side, j, t],
                    device_id={"blk": c, "uly": px}, device_id_type=MESH,
                ).start()

    diagonal = (
        lax.broadcasted_iota(jnp.int32, (rows, HD), 0)
        == lax.broadcasted_iota(jnp.int32, (rows, HD), 1)
    )
    chunk = ulys * rows
    for j in range(slots):
        await_bytes(kb.at[j], in_recv.at[j, 1])
        await_bytes(vb.at[j], in_recv.at[j, 2])
        for i in range(blocks):
            if i == 0:
                await_bytes(qb.at[j, side_rows(1 - side)], in_recv.at[j, 3])
            if i == half:
                await_bytes(qb.at[j, side_rows(side)], in_recv.at[j, 0])
            c = jnp.where(z < half, blocks - 1 - i, i)
            span = pl.ds(pl.multiple_of(c * chunk, chunk), chunk)
            scores = lax.dot_general(
                qb[j, span, :], kb[j], (((1,), (1,)), ((), ())),
                preferred_element_type=jnp.float32,
            )
            top = jnp.max(scores, axis=1, keepdims=True)
            weights = jnp.exp2((scores - top) * fold)
            totals = jnp.sum(weights, axis=1, keepdims=True)
            mixed = jnp.dot(
                weights.astype(jnp.bfloat16), vb[j], preferred_element_type=jnp.float32
            )
            ob[j, span, :] = (mixed / totals).astype(jnp.bfloat16)
            level = top * fold + jnp.log2(totals)
            for px in range(ulys):
                part = level[px * rows:(px + 1) * rows]
                sb[j, c * ulys + px] = jnp.sum(
                    jnp.where(diagonal, part, 0.0), axis=0, keepdims=True
                )
            for px in range(ulys):
                send_output(j, c, px)

    for j in range(slots):
        for s in range(2):
            await_bytes(ib.at[s, j], out_recv.at[s, j, 0])
            await_bytes(tb.at[s, j], out_recv.at[s, j, 1])
        for r in range(owners):
            share = 1.0 / (1.0 + jnp.exp2(tb[1, j, r] - tb[0, j, r]))
            share = jnp.sum(jnp.where(diagonal, share, 0.0), axis=1, keepdims=True)
            first = ib[0, j, r].astype(jnp.float32)
            second = ib[1, j, r].astype(jnp.float32)
            merged = second + share * (first - second)
            o_ref[0, :, pl.ds((r * slots + j) * HD, HD)] = merged.astype(jnp.bfloat16)

    others = blocks * ulys - 1
    for j in range(slots):
        await_bytes(qb.at[j, pl.ds(0, others * rows)], in_send.at[j, 0])
        await_bytes(kb.at[j, pl.ds(0, (owners - 1) * rows)], in_send.at[j, 1])
        await_bytes(vb.at[j, pl.ds(0, (owners - 1) * rows)], in_send.at[j, 2])
        await_bytes(ob.at[j, pl.ds(0, others * rows)], out_send.at[j, 0])
        await_bytes(sb.at[j, pl.ds(0, others)], out_send.at[j, 1])


def exchanged(query_rows, key_rows, value_rows):
    blocks = lax.axis_size("blk")
    ulys = lax.axis_size("uly")
    unused, rows, width = query_rows.shape
    heads = width // HD
    owners = blocks // 2 * ulys
    slots = heads // owners
    total = blocks * ulys * rows
    near = owners * rows
    return pl.pallas_call(
        functools.partial(exchange_kernel, blocks, ulys, rows, heads),
        out_shape=pltpu.VMEM(query_rows.shape, jnp.bfloat16),
        in_specs=[pl.BlockSpec(memory_space=pl.ANY)] * 3,
        out_specs=pl.BlockSpec(memory_space=pltpu.VMEM),
        scratch_shapes=[
            pltpu.VMEM((slots, total, HD), jnp.bfloat16),
            pltpu.VMEM((slots, near, HD), jnp.bfloat16),
            pltpu.VMEM((slots, near, HD), jnp.bfloat16),
            pltpu.VMEM((slots, total, HD), jnp.bfloat16),
            pltpu.VMEM((slots, blocks * ulys, 1, HD), jnp.float32),
            pltpu.VMEM((2, slots, owners, rows, HD), jnp.bfloat16),
            pltpu.VMEM((2, slots, owners, 1, HD), jnp.float32),
            pltpu.SemaphoreType.DMA((slots, 3)),
            pltpu.SemaphoreType.DMA((slots, 4)),
            pltpu.SemaphoreType.DMA((slots, 2)),
            pltpu.SemaphoreType.DMA((2, slots, 2)),
            pltpu.SemaphoreType.REGULAR((blocks,)),
        ],
        compiler_params=pltpu.CompilerParams(collective_id=0, has_side_effects=True),
    )(query_rows, key_rows, value_rows)


def local(query_rows, key_rows, value_rows):
    blocks = lax.axis_size("blk")
    ulys = lax.axis_size("uly")
    rows = query_rows.shape[1]
    heads = query_rows.shape[2] // HD
    tokens = rows * blocks * ulys
    even = blocks % 2 == 0 and heads % (blocks // 2 * ulys) == 0
    if even and tokens <= 1024 and rows <= HD and rows % 16 == 0:
        return exchanged(query_rows, key_rows, value_rows)
    return gathered(query_rows, key_rows, value_rows)


def solution(mesh):
    spec = P("cfg", ("groups", "blk", "uly"), None)
    return jax.shard_map(
        local, mesh=mesh, in_specs=(spec, spec, spec), out_specs=spec, check_vma=False
    )
```

```python
import functools
import math

import jax
import jax.numpy as jnp
from jax import lax
from jax.experimental import pallas as pl
from jax.experimental.pallas import tpu as pltpu
from jax.sharding import PartitionSpec as P

HD = 128
MESH = pl.DeviceIdType.MESH


def attend(queries, key_part, value_part):
    query_mat = queries[0, :, 0]
    row_count, head_count, head_size = query_mat.shape
    score_scale = 1.0 / math.sqrt(head_size)
    start_state = (
        jnp.full((head_count, row_count), -1e30, jnp.float32),
        jnp.zeros((head_count, row_count), jnp.float32),
        jnp.zeros((row_count, head_count, head_size), jnp.float32),
    )

    def absorb(state, pieces):
        key_piece = pieces[0][0, :, 0]
        value_piece = pieces[1][0, :, 0]
        scores = (
            jnp.einsum("qhd,khd->hqk", query_mat, key_piece, preferred_element_type=jnp.float32)
            * score_scale
        )
        running, totals, accumulated = state
        new_max = jnp.maximum(running, jnp.max(scores, axis=2))
        weights = jnp.exp(scores - new_max[:, :, None])
        factor = jnp.exp(running - new_max)
        totals = totals * factor + jnp.sum(weights, axis=2)
        probabilities = weights.astype(jnp.bfloat16)
        contrib = jnp.einsum(
            "hqk,khd->qhd", probabilities, value_piece, preferred_element_type=jnp.float32
        )
        accumulated = accumulated * factor.T[:, :, None] + contrib
        return (new_max, totals, accumulated)

    whole_keys, whole_values = (
        lax.all_gather(key_part, "blk", axis=1, tiled=True),
        lax.all_gather(value_part, "blk", axis=1, tiled=True),
    )
    key_count = whole_keys.shape[1]
    block_rows = math.gcd(key_count, 1024)

    def one_block(state, counter):
        offset = counter * block_rows
        key_block = lax.dynamic_slice_in_dim(whole_keys, offset, block_rows, 1)
        value_block = lax.dynamic_slice_in_dim(whole_values, offset, block_rows, 1)
        return (absorb(state, (key_block, value_block)), None)

    result, unused = lax.scan(
        one_block, start_state, jnp.arange(key_count // block_rows, dtype=jnp.int32)
    )
    output = (result[2] / result[1].T[:, :, None]).astype(jnp.bfloat16)
    return output.reshape(1, row_count, 1, head_count, head_size)


def gathered(query_rows, key_rows, value_rows):
    ulysses = lax.axis_size("uly")
    tokens = query_rows.shape[1]
    width = query_rows.shape[2]
    heads_local = width // HD // ulysses

    def moved(array):
        sections = array.reshape(1, tokens, ulysses, heads_local, HD)
        return lax.all_to_all(sections, "uly", split_axis=2, concat_axis=1, tiled=True)

    mixed = attend(moved(query_rows), moved(key_rows), moved(value_rows))
    merged = lax.all_to_all(mixed, "uly", split_axis=1, concat_axis=2, tiled=True)
    return merged.reshape(1, tokens, width)


def head_counts(heads_column, blocks):
    counts = [heads_column // blocks] * blocks
    by_middle = sorted(range(blocks), key=lambda z: (abs(2 * z - (blocks - 1)), z))
    for z in by_middle[: heads_column % blocks]:
        counts[z] += 1
    return counts


def exchange_kernel(
    blocks, ulys, rows, heads, q_ref, k_ref, v_ref, o_ref,
    qb, kb, vb, pb, ob, in_send, in_recv, out_send, out_recv, row_in,
):
    peers = blocks * ulys
    column = heads // ulys
    counts = head_counts(column, blocks)
    starts = [sum(counts[:z]) for z in range(blocks)]
    slots = max(counts)
    z = lax.axis_index("blk")
    x = lax.axis_index("uly")
    me = z * ulys + x
    sources = (q_ref, k_ref, v_ref)
    buffers = (qb, kb, vb)
    fold = (1.0 / math.sqrt(HD)) * math.log2(math.e)
    chunk_rows = ulys * rows

    def first_of(pz):
        first = jnp.int32(0)
        for i in range(blocks):
            first = first + jnp.where(pz > i, counts[i], 0)
        return first

    def holds_at(pz, s):
        has = pz < 0
        for i in range(blocks):
            if counts[i] > s:
                has = jnp.logical_or(has, pz == i)
        return has

    my_head = x * column + first_of(z)
    my_rows = pl.ds(pl.multiple_of(me * rows, rows), rows)
    turn = jnp.where(z < blocks // 2, blocks // 2, 0)

    def piece(t, head):
        return sources[t].at[0, :, pl.ds(pl.multiple_of(head * HD, HD), HD)]

    def copy_to(s, t, pz, px):
        return pltpu.make_async_remote_copy(
            src_ref=piece(t, px * column + first_of(pz) + s),
            dst_ref=buffers[t].at[s, my_rows],
            send_sem=in_send.at[s, t, pz * ulys + px],
            recv_sem=in_recv.at[s, t, me],
            device_id={"blk": pz, "uly": px},
            device_id_type=MESH,
        )

    def send(s, pz, px):
        for t in range(3):
            copy_to(s, t, pz, px).start()

    def token(row, to):
        pl.semaphore_signal(
            row_in.at[row], inc=1, device_id={"blk": to, "uly": x}, device_id_type=MESH
        )

    def send_inputs(zz):
        half = blocks // 2
        toward = 1 if zz < half else -1
        sent = set()

        def crosses(pz):
            return pz // half != zz // half

        def give(s, pz, *turns):
            for e in turns:
                if counts[pz] > s and (pz != zz or e) and (s, pz, e) not in sent:
                    sent.add((s, pz, e))
                    send(s, pz, lax.rem(x + e, ulys))

        def hear(pz):
            pl.semaphore_wait(row_in.at[pz], 1)
            onward = zz - 1 if pz > zz else zz + 1
            if 0 <= onward < blocks:
                token(pz, onward)

        every = tuple(range(ulys))
        beside = [zz + e for e in (toward, -toward) if 0 <= zz + e < blocks]
        away = sorted((pz for pz in range(blocks) if crosses(pz)), key=lambda pz: -abs(pz - zz))
        mine = sorted((pz for pz in range(blocks) if not crosses(pz)), key=lambda pz: -abs(pz - zz))
        for pz in beside:
            token(zz, pz)
        for s in range(slots):
            for pz in beside:
                give(s, pz, 0)
        for s in range(slots):
            give(s, zz, *every)
        for d in range(1, blocks):
            for e in (toward, -toward):
                pz = zz + e * d
                if 0 <= pz < blocks:
                    hear(pz)
                    if crosses(pz):
                        give(0, pz, *every)
        for s in range(slots):
            for pz in away + mine:
                give(s, pz, *every)

    barrier = pltpu.get_barrier_semaphore()

    def greet(pz, px):
        pl.semaphore_signal(
            barrier, inc=1, device_id={"blk": pz, "uly": px}, device_id_type=MESH
        )

    pl.when(z > 0)(lambda: greet(z - 1, x))
    pl.when(z < blocks - 1)(lambda: greet(z + 1, x))
    for d in range(1, ulys):
        greet(z, lax.rem(x + d, ulys))
    def own(s):
        for t in range(3):
            pltpu.make_async_copy(
                piece(t, my_head + s), buffers[t].at[s, my_rows], in_recv.at[s, t, me]
            ).start()

    for s in range(slots):
        pl.when(holds_at(z, s))(functools.partial(own, s))
    greeted = (ulys - 1) + jnp.where(z > 0, 1, 0) + jnp.where(z < blocks - 1, 1, 0)
    pl.semaphore_wait(barrier, greeted)

    for zz in range(blocks):
        pl.when(z == zz)(functools.partial(send_inputs, zz))

    def landed(s, t):
        def one(p, carry):
            block = buffers[t].at[s, pl.ds(pl.multiple_of(p * rows, rows), rows)]
            pltpu.make_async_copy(block, block, in_recv.at[s, t, p]).wait()
            return carry

        lax.fori_loop(0, peers, one, 0)

    def out_copy(s, c, px):
        head = pl.multiple_of((my_head + s) * HD, HD)
        begin = pl.multiple_of((c * ulys + px) * rows, rows)
        return ob.at[s, pl.ds(begin, rows)], o_ref.at[0, :, pl.ds(head, HD)]

    def out_remote(s, c, px):
        src, dst = out_copy(s, c, px)
        return pltpu.make_async_remote_copy(
            src_ref=src, dst_ref=dst,
            send_sem=out_send.at[s, c * ulys + px],
            recv_sem=out_recv.at[my_head + s],
            device_id={"blk": c, "uly": px}, device_id_type=MESH,
        )

    def out_local(s, c, px):
        src, dst = out_copy(s, c, px)
        return pltpu.make_async_copy(src, dst, out_recv.at[my_head + s])

    late = jnp.logical_and(lax.axis_index("cfg") == 1, holds_at(z, slots - 1))

    def send_output(s, c):
        for px in range(ulys):
            mine = jnp.logical_and(c == z, x == px)

            @pl.when(mine)
            def _():
                out_local(s, c, px).start()

            @pl.when(jnp.logical_not(mine))
            def _():
                out_remote(s, c, px).start()

    def send_late():
        for s in range(slots - 1):
            for i in range((blocks + 1) // 2):
                send_output(s, jnp.where(z < blocks // 2, blocks - 1 - i, i))

    def one_slot(s):
        landed(s, 0)
        landed(s, 1)
        totals = []
        for i in range(blocks):
            c = jnp.where(z < blocks // 2, blocks - 1 - i, i)
            span = pl.ds(pl.multiple_of(c * chunk_rows, chunk_rows), chunk_rows)
            scores = lax.dot_general(
                qb[s, span, :], kb[s], (((1,), (1,)), ((), ())),
                preferred_element_type=jnp.float32,
            )
            top = jnp.max(scores, axis=1, keepdims=True)
            weights = jnp.exp2((scores - top) * fold)
            totals.append(jnp.sum(weights, axis=1, keepdims=True))
            pb[span, :] = weights.astype(jnp.bfloat16)
        landed(s, 2)
        if s > 0 and s == slots - 1:
            pl.when(late)(send_late)
        for i in range(blocks):
            c = jnp.where(z < blocks // 2, blocks - 1 - i, i)
            span = pl.ds(pl.multiple_of(c * chunk_rows, chunk_rows), chunk_rows)
            mixed = jnp.dot(pb[span, :], vb[s], preferred_element_type=jnp.float32)
            ob[s, span, :] = (mixed / totals[i]).astype(jnp.bfloat16)
            if s < slots - 1 and 2 * i < blocks:
                pl.when(jnp.logical_not(late))(functools.partial(send_output, s, c))
            else:
                send_output(s, c)

    for s in range(slots):
        if min(counts) > s:
            one_slot(s)
        else:
            pl.when(holds_at(z, s))(functools.partial(one_slot, s))

    def result_landed(head, carry):
        block = o_ref.at[0, :, pl.ds(pl.multiple_of(head * HD, HD), HD)]
        pltpu.make_async_copy(block, block, out_recv.at[head]).wait()
        return carry

    def all_sent(p, carry):
        pz, px = p // ulys, lax.rem(p, ulys)
        for s in range(slots):
            @pl.when(jnp.logical_and(p != me, holds_at(pz, s)))
            def _():
                for t in range(3):
                    copy_to(s, t, pz, px).wait_send()

            @pl.when(jnp.logical_and(p != me, holds_at(z, s)))
            def _():
                out_remote(s, pz, px).wait_send()
        return carry

    lax.fori_loop(0, peers, all_sent, 0)
    lax.fori_loop(0, heads, result_landed, 0)


def exchanged(query_rows, key_rows, value_rows):
    blocks = lax.axis_size("blk")
    ulys = lax.axis_size("uly")
    unused, rows, width = query_rows.shape
    heads = width // HD
    peers = blocks * ulys
    slots = max(head_counts(heads // ulys, blocks))
    total = peers * rows
    return pl.pallas_call(
        functools.partial(exchange_kernel, blocks, ulys, rows, heads),
        out_shape=pltpu.VMEM(query_rows.shape, jnp.bfloat16),
        in_specs=[pl.BlockSpec(memory_space=pl.ANY)] * 3,
        out_specs=pl.BlockSpec(memory_space=pltpu.VMEM),
        scratch_shapes=[
            pltpu.VMEM((slots, total, HD), jnp.bfloat16),
            pltpu.VMEM((slots, total, HD), jnp.bfloat16),
            pltpu.VMEM((slots, total, HD), jnp.bfloat16),
            pltpu.VMEM((total, total), jnp.bfloat16),
            pltpu.VMEM((slots, total, HD), jnp.bfloat16),
            pltpu.SemaphoreType.DMA((slots, 3, peers)),
            pltpu.SemaphoreType.DMA((slots, 3, peers)),
            pltpu.SemaphoreType.DMA((slots, peers)),
            pltpu.SemaphoreType.DMA((heads,)),
            pltpu.SemaphoreType.REGULAR((blocks,)),
        ],
        compiler_params=pltpu.CompilerParams(collective_id=0, has_side_effects=True),
    )(query_rows, key_rows, value_rows)


def local(query_rows, key_rows, value_rows):
    blocks = lax.axis_size("blk")
    ulys = lax.axis_size("uly")
    heads = query_rows.shape[2] // HD
    tokens = query_rows.shape[1] * blocks * ulys
    if heads % ulys == 0 and heads // ulys >= blocks and tokens <= 1024:
        return exchanged(query_rows, key_rows, value_rows)
    return gathered(query_rows, key_rows, value_rows)


def solution(mesh):
    spec = P("cfg", ("groups", "blk", "uly"), None)
    return jax.shard_map(
        local, mesh=mesh, in_specs=(spec, spec, spec), out_specs=spec, check_vma=False
    )
```

```python
import functools
import math

import jax
import jax.numpy as jnp
from jax import lax
from jax.experimental import pallas as pl
from jax.experimental.pallas import tpu as pltpu
from jax.sharding import PartitionSpec as P

HD = 128
MESH = pl.DeviceIdType.MESH


def attend(queries, key_part, value_part):
    query_mat = queries[0, :, 0]
    row_count, head_count, head_size = query_mat.shape
    score_scale = 1.0 / math.sqrt(head_size)
    start_state = (
        jnp.full((head_count, row_count), -1e30, jnp.float32),
        jnp.zeros((head_count, row_count), jnp.float32),
        jnp.zeros((row_count, head_count, head_size), jnp.float32),
    )

    def absorb(state, pieces):
        key_piece = pieces[0][0, :, 0]
        value_piece = pieces[1][0, :, 0]
        scores = (
            jnp.einsum("qhd,khd->hqk", query_mat, key_piece, preferred_element_type=jnp.float32)
            * score_scale
        )
        running, totals, accumulated = state
        new_max = jnp.maximum(running, jnp.max(scores, axis=2))
        weights = jnp.exp(scores - new_max[:, :, None])
        factor = jnp.exp(running - new_max)
        totals = totals * factor + jnp.sum(weights, axis=2)
        probabilities = weights.astype(jnp.bfloat16)
        contrib = jnp.einsum(
            "hqk,khd->qhd", probabilities, value_piece, preferred_element_type=jnp.float32
        )
        accumulated = accumulated * factor.T[:, :, None] + contrib
        return (new_max, totals, accumulated)

    whole_keys, whole_values = (
        lax.all_gather(key_part, "blk", axis=1, tiled=True),
        lax.all_gather(value_part, "blk", axis=1, tiled=True),
    )
    key_count = whole_keys.shape[1]
    block_rows = math.gcd(key_count, 1024)

    def one_block(state, counter):
        offset = counter * block_rows
        key_block = lax.dynamic_slice_in_dim(whole_keys, offset, block_rows, 1)
        value_block = lax.dynamic_slice_in_dim(whole_values, offset, block_rows, 1)
        return (absorb(state, (key_block, value_block)), None)

    result, unused = lax.scan(
        one_block, start_state, jnp.arange(key_count // block_rows, dtype=jnp.int32)
    )
    output = (result[2] / result[1].T[:, :, None]).astype(jnp.bfloat16)
    return output.reshape(1, row_count, 1, head_count, head_size)


def gathered(query_rows, key_rows, value_rows):
    ulysses = lax.axis_size("uly")
    tokens = query_rows.shape[1]
    width = query_rows.shape[2]
    heads_local = width // HD // ulysses

    def moved(array):
        sections = array.reshape(1, tokens, ulysses, heads_local, HD)
        return lax.all_to_all(sections, "uly", split_axis=2, concat_axis=1, tiled=True)

    mixed = attend(moved(query_rows), moved(key_rows), moved(value_rows))
    merged = lax.all_to_all(mixed, "uly", split_axis=1, concat_axis=2, tiled=True)
    return merged.reshape(1, tokens, width)


def exchange_kernel(
    blocks, ulys, rows, q_ref, k_ref, v_ref, o_ref,
    qf, kf, vf, of, qs, ks, vs, os, sb, ib, tb,
    in_send, in_recv, out_send, out_recv, row_in,
):
    half = blocks // 2
    owners = half * ulys
    peers = blocks * ulys
    near = owners * rows
    chunk = ulys * rows
    z = lax.axis_index("blk")
    x = lax.axis_index("uly")
    me = z * ulys + x
    side = z // half
    lead = lax.axis_index("cfg") == 0
    rank = lax.rem(me, owners)
    sources = (q_ref, k_ref, v_ref)
    wholes = (qf, kf, vf)
    shared = (qs, ks, vs)
    fold = (1.0 / math.sqrt(HD)) * math.log2(math.e)

    def part(begin, size):
        return pl.ds(pl.multiple_of(begin, size), size)

    def whole_copy(t, to):
        return (
            sources[t].at[0, :, part(to * HD, HD)],
            wholes[t].at[part(me * rows, rows)],
        )

    def shared_copy(t, to):
        begin = (me if t == 0 else rank) * rows
        return (
            sources[t].at[0, :, part((peers + lax.rem(to, owners)) * HD, HD)],
            shared[t].at[part(begin, rows)],
        )

    def remote(copy, sent, landed, pz, px):
        pltpu.make_async_remote_copy(
            src_ref=copy[0], dst_ref=copy[1], send_sem=sent, recv_sem=landed,
            device_id={"blk": pz, "uly": px}, device_id_type=MESH,
        ).start()

    def send(kind, pz, px, crosses):
        to = pz * ulys + px
        for t in range(3):
            if kind == 0:
                remote(whole_copy(t, to), in_send.at[0, t], in_recv.at[t], pz, px)
            elif t == 0 or not crosses:
                landed = in_recv.at[6 if crosses else 3 + t]
                remote(shared_copy(t, to), in_send.at[1, t], landed, pz, px)

    barrier = pltpu.get_barrier_semaphore()

    def greet(pz, px):
        pl.semaphore_signal(
            barrier, inc=1, device_id={"blk": pz, "uly": px}, device_id_type=MESH
        )

    pl.when(z > 0)(lambda: greet(z - 1, x))
    pl.when(z < blocks - 1)(lambda: greet(z + 1, x))
    for d in range(1, ulys):
        greet(z, lax.rem(x + d, ulys))
    for t in range(3):
        pltpu.make_async_copy(*whole_copy(t, me), in_recv.at[t]).start()
        pltpu.make_async_copy(*shared_copy(t, me), in_recv.at[3 + t]).start()
    greeted = (ulys - 1) + jnp.where(z > 0, 1, 0) + jnp.where(z < blocks - 1, 1, 0)
    pl.semaphore_wait(barrier, greeted)

    def token(row, to):
        pl.semaphore_signal(
            row_in.at[row], inc=1, device_id={"blk": to, "uly": x}, device_id_type=MESH
        )

    def send_inputs(zz):
        toward = 1 if zz < half else -1
        sent = set()

        def crosses(pz):
            return pz // half != zz // half

        def give(kind, pz, *turns):
            for e in turns:
                if (pz != zz or e) and (kind, pz, e) not in sent:
                    sent.add((kind, pz, e))
                    send(kind, pz, lax.rem(x + e, ulys), crosses(pz))

        def hear(pz):
            pl.semaphore_wait(row_in.at[pz], 1)
            onward = zz - 1 if pz > zz else zz + 1
            if 0 <= onward < blocks:
                token(pz, onward)

        every = tuple(range(ulys))
        beside = [zz + e for e in (toward, -toward) if 0 <= zz + e < blocks]
        away = sorted((pz for pz in range(blocks) if crosses(pz)), key=lambda pz: -abs(pz - zz))
        mine = sorted((pz for pz in range(blocks) if not crosses(pz)), key=lambda pz: -abs(pz - zz))
        for pz in beside:
            token(zz, pz)
        for kind in range(2):
            for pz in beside:
                give(kind, pz, 0)
        for kind in range(2):
            give(kind, zz, *every)
        for d in range(1, blocks):
            for e in (toward, -toward):
                pz = zz + e * d
                if 0 <= pz < blocks:
                    hear(pz)
                    if crosses(pz):
                        give(0, pz, *every)
        for kind in range(2):
            for pz in away + mine:
                give(kind, pz, *every)

    for zz in range(blocks):
        pl.when(z == zz)(functools.partial(send_inputs, zz))

    def await_bytes(ref, sem):
        pltpu.make_async_copy(ref, ref, sem).wait()

    def row_of(i):
        return jnp.where(z < half, blocks - 1 - i, i)

    def deliver(copies, c, px):
        own = c * ulys + px == me

        @pl.when(own)
        def _():
            for src, dst, sent, landed in copies:
                pltpu.make_async_copy(src, dst, landed).start()

        @pl.when(jnp.logical_not(own))
        def _():
            for src, dst, sent, landed in copies:
                remote((src, dst), sent, landed, c, px)

    def send_whole(i):
        c = row_of(i)
        for px in range(ulys):
            src = of.at[part((c * ulys + px) * rows, rows)]
            dst = o_ref.at[0, :, part(me * HD, HD)]
            deliver(((src, dst, out_send.at[0], out_recv.at[0]),), c, px)

    def send_shared(i):
        c = row_of(i)
        for px in range(ulys):
            to = c * ulys + px
            deliver((
                (os.at[part(to * rows, rows)], ib.at[side, rank], out_send.at[1], out_recv.at[1 + side]),
                (sb.at[to], tb.at[side, rank], out_send.at[2], out_recv.at[3 + side]),
            ), c, px)

    def attention(q, k, v):
        scores = lax.dot_general(
            q, k, (((1,), (1,)), ((), ())), preferred_element_type=jnp.float32
        )
        top = jnp.max(scores, axis=1, keepdims=True)
        weights = jnp.exp2((scores - top) * fold)
        totals = jnp.sum(weights, axis=1, keepdims=True)
        mixed = jnp.dot(weights.astype(jnp.bfloat16), v, preferred_element_type=jnp.float32)
        return (mixed / totals).astype(jnp.bfloat16), top * fold + jnp.log2(totals)

    for t in range(3):
        await_bytes(wholes[t], in_recv.at[t])
    for i in range(blocks):
        span = part(row_of(i) * chunk, chunk)
        of[span, :] = attention(qf[span, :], kf[...], vf[...])[0]
        if i >= half:
            send_whole(i)
        elif i == 0:
            pl.when(lead)(functools.partial(send_whole, i))

    diagonal = (
        lax.broadcasted_iota(jnp.int32, (rows, HD), 0)
        == lax.broadcasted_iota(jnp.int32, (rows, HD), 1)
    )
    await_bytes(ks, in_recv.at[4])
    await_bytes(vs, in_recv.at[5])
    await_bytes(qs.at[part((1 - side) * near, near)], in_recv.at[6])
    for i in range(blocks):
        if i == half:
            await_bytes(qs.at[part(side * near, near)], in_recv.at[3])
        c = row_of(i)
        span = part(c * chunk, chunk)
        mixed, level = attention(qs[span, :], ks[...], vs[...])
        os[span, :] = mixed
        for px in range(ulys):
            sb[c * ulys + px] = jnp.sum(
                jnp.where(diagonal, level[px * rows:(px + 1) * rows], 0.0), axis=0, keepdims=True
            )
        if i == half:
            for k in range(half):
                pl.when(jnp.logical_not(lead))(functools.partial(send_whole, k))
        send_shared(i)
        if i == 0:
            for k in range(1, half):
                pl.when(lead)(functools.partial(send_whole, k))

    for s in range(2):
        await_bytes(ib.at[s], out_recv.at[1 + s])
        await_bytes(tb.at[s], out_recv.at[3 + s])
    for r in range(owners):
        share = 1.0 / (1.0 + jnp.exp2(tb[1, r] - tb[0, r]))
        share = jnp.sum(jnp.where(diagonal, share, 0.0), axis=1, keepdims=True)
        first = ib[0, r].astype(jnp.float32)
        second = ib[1, r].astype(jnp.float32)
        merged = second + share * (first - second)
        o_ref[0, :, pl.ds((peers + r) * HD, HD)] = merged.astype(jnp.bfloat16)
    await_bytes(o_ref.at[0, :, pl.ds(0, peers * HD)], out_recv.at[0])

    for t in range(3):
        await_bytes(wholes[t].at[pl.ds(0, (peers - 1) * rows)], in_send.at[0, t])
        others = (peers if t == 0 else owners) - 1
        await_bytes(shared[t].at[pl.ds(0, others * rows)], in_send.at[1, t])
    await_bytes(of.at[pl.ds(0, (peers - 1) * rows)], out_send.at[0])
    await_bytes(os.at[pl.ds(0, (peers - 1) * rows)], out_send.at[1])
    await_bytes(sb.at[pl.ds(0, peers - 1)], out_send.at[2])


def exchanged(query_rows, key_rows, value_rows):
    blocks = lax.axis_size("blk")
    ulys = lax.axis_size("uly")
    rows = query_rows.shape[1]
    owners = blocks // 2 * ulys
    peers = blocks * ulys
    full = pltpu.VMEM((peers * rows, HD), jnp.bfloat16)
    less = pltpu.VMEM((owners * rows, HD), jnp.bfloat16)
    return pl.pallas_call(
        functools.partial(exchange_kernel, blocks, ulys, rows),
        out_shape=pltpu.VMEM(query_rows.shape, jnp.bfloat16),
        in_specs=[pl.BlockSpec(memory_space=pl.ANY)] * 3,
        out_specs=pl.BlockSpec(memory_space=pltpu.VMEM),
        scratch_shapes=[
            full, full, full, full, full, less, less, full,
            pltpu.VMEM((peers, 1, HD), jnp.float32),
            pltpu.VMEM((2, owners, rows, HD), jnp.bfloat16),
            pltpu.VMEM((2, owners, 1, HD), jnp.float32),
            pltpu.SemaphoreType.DMA((2, 3)),
            pltpu.SemaphoreType.DMA((7,)),
            pltpu.SemaphoreType.DMA((3,)),
            pltpu.SemaphoreType.DMA((5,)),
            pltpu.SemaphoreType.REGULAR((blocks,)),
        ],
        compiler_params=pltpu.CompilerParams(collective_id=0, has_side_effects=True),
    )(query_rows, key_rows, value_rows)


def local(query_rows, key_rows, value_rows):
    blocks = lax.axis_size("blk")
    ulys = lax.axis_size("uly")
    rows = query_rows.shape[1]
    heads = query_rows.shape[2] // HD
    peers = blocks * ulys
    even = blocks % 2 == 0 and 2 * heads == 3 * peers
    if even and rows * peers <= 1024 and rows <= HD and rows % 16 == 0:
        return exchanged(query_rows, key_rows, value_rows)
    return gathered(query_rows, key_rows, value_rows)


def solution(mesh):
    spec = P("cfg", ("groups", "blk", "uly"), None)
    return jax.shard_map(
        local, mesh=mesh, in_specs=(spec, spec, spec), out_specs=spec, check_vma=False
    )
```

```python
import functools
import math

import jax
import jax.numpy as jnp
from jax import lax
from jax.experimental import pallas as pl
from jax.experimental.pallas import tpu as pltpu
from jax.sharding import PartitionSpec as P

HD = 128
MESH = pl.DeviceIdType.MESH


def attend(queries, key_part, value_part):
    query_mat = queries[0, :, 0]
    row_count, head_count, head_size = query_mat.shape
    score_scale = 1.0 / math.sqrt(head_size)
    start_state = (
        jnp.full((head_count, row_count), -1e30, jnp.float32),
        jnp.zeros((head_count, row_count), jnp.float32),
        jnp.zeros((row_count, head_count, head_size), jnp.float32),
    )

    def absorb(state, pieces):
        key_piece = pieces[0][0, :, 0]
        value_piece = pieces[1][0, :, 0]
        scores = (
            jnp.einsum("qhd,khd->hqk", query_mat, key_piece, preferred_element_type=jnp.float32)
            * score_scale
        )
        running, totals, accumulated = state
        new_max = jnp.maximum(running, jnp.max(scores, axis=2))
        weights = jnp.exp(scores - new_max[:, :, None])
        factor = jnp.exp(running - new_max)
        totals = totals * factor + jnp.sum(weights, axis=2)
        probabilities = weights.astype(jnp.bfloat16)
        contrib = jnp.einsum(
            "hqk,khd->qhd", probabilities, value_piece, preferred_element_type=jnp.float32
        )
        accumulated = accumulated * factor.T[:, :, None] + contrib
        return (new_max, totals, accumulated)

    whole_keys, whole_values = (
        lax.all_gather(key_part, "blk", axis=1, tiled=True),
        lax.all_gather(value_part, "blk", axis=1, tiled=True),
    )
    key_count = whole_keys.shape[1]
    block_rows = math.gcd(key_count, 1024)

    def one_block(state, counter):
        offset = counter * block_rows
        key_block = lax.dynamic_slice_in_dim(whole_keys, offset, block_rows, 1)
        value_block = lax.dynamic_slice_in_dim(whole_values, offset, block_rows, 1)
        return (absorb(state, (key_block, value_block)), None)

    result, unused = lax.scan(
        one_block, start_state, jnp.arange(key_count // block_rows, dtype=jnp.int32)
    )
    output = (result[2] / result[1].T[:, :, None]).astype(jnp.bfloat16)
    return output.reshape(1, row_count, 1, head_count, head_size)


def gathered(query_rows, key_rows, value_rows):
    ulysses = lax.axis_size("uly")
    tokens = query_rows.shape[1]
    width = query_rows.shape[2]
    heads_local = width // HD // ulysses

    def moved(array):
        sections = array.reshape(1, tokens, ulysses, heads_local, HD)
        return lax.all_to_all(sections, "uly", split_axis=2, concat_axis=1, tiled=True)

    mixed = attend(moved(query_rows), moved(key_rows), moved(value_rows))
    merged = lax.all_to_all(mixed, "uly", split_axis=1, concat_axis=2, tiled=True)
    return merged.reshape(1, tokens, width)


def exchange_kernel(
    blocks, ulys, rows, q_ref, k_ref, v_ref, o_ref,
    qf, kf, vf, of, qs, ks, vs, os, sb, ib, tb,
    in_send, in_recv, out_send, out_recv, row_in,
):
    half = blocks // 2
    owners = half * ulys
    peers = blocks * ulys
    near = owners * rows
    chunk = ulys * rows
    z = lax.axis_index("blk")
    x = lax.axis_index("uly")
    me = z * ulys + x
    side = z // half
    lead = lax.axis_index("cfg") == 0
    rank = lax.rem(me, owners)
    sources = (q_ref, k_ref, v_ref)
    wholes = (qf, kf, vf)
    shared = (qs, ks, vs)
    fold = (1.0 / math.sqrt(HD)) * math.log2(math.e)

    def part(begin, size):
        return pl.ds(pl.multiple_of(begin, size), size)

    def whole_copy(t, to):
        return (
            sources[t].at[0, :, part(to * HD, HD)],
            wholes[t].at[part(me * rows, rows)],
        )

    def shared_copy(t, to):
        begin = (me if t == 0 else rank) * rows
        return (
            sources[t].at[0, :, part((peers + lax.rem(to, owners)) * HD, HD)],
            shared[t].at[part(begin, rows)],
        )

    def remote(copy, sent, landed, pz, px):
        pltpu.make_async_remote_copy(
            src_ref=copy[0], dst_ref=copy[1], send_sem=sent, recv_sem=landed,
            device_id={"blk": pz, "uly": px}, device_id_type=MESH,
        ).start()

    def send(kind, pz, px, crosses):
        to = pz * ulys + px
        for t in range(3):
            if kind == 0:
                remote(whole_copy(t, to), in_send.at[0, t], in_recv.at[t], pz, px)
            elif t == 0 or not crosses:
                landed = in_recv.at[6 if crosses else 3 + t]
                remote(shared_copy(t, to), in_send.at[1, t], landed, pz, px)

    barrier = pltpu.get_barrier_semaphore()

    def greet(pz, px):
        pl.semaphore_signal(
            barrier, inc=1, device_id={"blk": pz, "uly": px}, device_id_type=MESH
        )

    pl.when(z > 0)(lambda: greet(z - 1, x))
    pl.when(z < blocks - 1)(lambda: greet(z + 1, x))
    for d in range(1, ulys):
        greet(z, lax.rem(x + d, ulys))
    for t in range(3):
        pltpu.make_async_copy(*whole_copy(t, me), in_recv.at[t]).start()
        pltpu.make_async_copy(*shared_copy(t, me), in_recv.at[3 + t]).start()
    greeted = (ulys - 1) + jnp.where(z > 0, 1, 0) + jnp.where(z < blocks - 1, 1, 0)
    pl.semaphore_wait(barrier, greeted)

    def token(row, to):
        pl.semaphore_signal(
            row_in.at[row], inc=1, device_id={"blk": to, "uly": x}, device_id_type=MESH
        )

    def send_inputs(zz):
        toward = 1 if zz < half else -1
        sent = set()

        def crosses(pz):
            return pz // half != zz // half

        def give(kind, pz, *turns):
            for e in turns:
                if (pz != zz or e) and (kind, pz, e) not in sent:
                    sent.add((kind, pz, e))
                    send(kind, pz, lax.rem(x + e, ulys), crosses(pz))

        def hear(pz):
            pl.semaphore_wait(row_in.at[pz], 1)
            onward = zz - 1 if pz > zz else zz + 1
            if 0 <= onward < blocks:
                token(pz, onward)

        every = tuple(range(ulys))
        beside = [zz + e for e in (toward, -toward) if 0 <= zz + e < blocks]
        away = sorted((pz for pz in range(blocks) if crosses(pz)), key=lambda pz: -abs(pz - zz))
        mine = sorted((pz for pz in range(blocks) if not crosses(pz)), key=lambda pz: -abs(pz - zz))
        for pz in beside:
            token(zz, pz)
        for kind in range(2):
            for pz in beside:
                give(kind, pz, 0)
        for kind in range(2):
            give(kind, zz, *every)
        for d in range(1, blocks):
            for e in (toward, -toward):
                pz = zz + e * d
                if 0 <= pz < blocks:
                    hear(pz)
                    outward = abs(2 * pz - blocks + 1) > abs(2 * zz - blocks + 1)
                    if crosses(pz) or outward:
                        give(0, pz, *every)
        for kind in range(2):
            for pz in away + mine:
                give(kind, pz, *every)

    for zz in range(blocks):
        pl.when(z == zz)(functools.partial(send_inputs, zz))

    def await_bytes(ref, sem):
        pltpu.make_async_copy(ref, ref, sem).wait()

    def row_of(i):
        return jnp.where(z < half, blocks - 1 - i, i)

    def deliver(copies, c, px):
        own = c * ulys + px == me

        @pl.when(own)
        def _():
            for src, dst, sent, landed in copies:
                pltpu.make_async_copy(src, dst, landed).start()

        @pl.when(jnp.logical_not(own))
        def _():
            for src, dst, sent, landed in copies:
                remote((src, dst), sent, landed, c, px)

    def send_whole(i):
        c = row_of(i)
        for px in range(ulys):
            src = of.at[part((c * ulys + px) * rows, rows)]
            dst = o_ref.at[0, :, part(me * HD, HD)]
            deliver(((src, dst, out_send.at[0], out_recv.at[0]),), c, px)

    def send_shared(i):
        c = row_of(i)
        for px in range(ulys):
            to = c * ulys + px
            deliver((
                (os.at[part(to * rows, rows)], ib.at[side, rank], out_send.at[1], out_recv.at[1 + side]),
                (sb.at[to], tb.at[side, rank], out_send.at[2], out_recv.at[3 + side]),
            ), c, px)

    def attention(q, k, v):
        scores = lax.dot_general(
            q, k, (((1,), (1,)), ((), ())), preferred_element_type=jnp.float32
        )
        top = jnp.max(scores, axis=1, keepdims=True)
        weights = jnp.exp2((scores - top) * fold)
        totals = jnp.sum(weights, axis=1, keepdims=True)
        mixed = jnp.dot(weights.astype(jnp.bfloat16), v, preferred_element_type=jnp.float32)
        return (mixed / totals).astype(jnp.bfloat16), top * fold + jnp.log2(totals)

    for t in range(3):
        await_bytes(wholes[t], in_recv.at[t])
    for i in range(blocks):
        span = part(row_of(i) * chunk, chunk)
        of[span, :] = attention(qf[span, :], kf[...], vf[...])[0]
        if i >= half:
            send_whole(i)
        elif i == 0:
            pl.when(lead)(functools.partial(send_whole, i))

    diagonal = (
        lax.broadcasted_iota(jnp.int32, (rows, HD), 0)
        == lax.broadcasted_iota(jnp.int32, (rows, HD), 1)
    )
    await_bytes(ks, in_recv.at[4])
    await_bytes(vs, in_recv.at[5])
    await_bytes(qs.at[part((1 - side) * near, near)], in_recv.at[6])
    for i in range(blocks):
        if i == half:
            await_bytes(qs.at[part(side * near, near)], in_recv.at[3])
        c = row_of(i)
        span = part(c * chunk, chunk)
        mixed, level = attention(qs[span, :], ks[...], vs[...])
        os[span, :] = mixed
        for px in range(ulys):
            sb[c * ulys + px] = jnp.sum(
                jnp.where(diagonal, level[px * rows:(px + 1) * rows], 0.0), axis=0, keepdims=True
            )
        if i == half:
            for k in range(half):
                pl.when(jnp.logical_not(lead))(functools.partial(send_whole, k))
        send_shared(i)
        if i == 0:
            for k in range(1, half):
                pl.when(lead)(functools.partial(send_whole, k))

    for s in range(2):
        await_bytes(ib.at[s], out_recv.at[1 + s])
        await_bytes(tb.at[s], out_recv.at[3 + s])
    for r in range(owners):
        share = 1.0 / (1.0 + jnp.exp2(tb[1, r] - tb[0, r]))
        share = jnp.sum(jnp.where(diagonal, share, 0.0), axis=1, keepdims=True)
        first = ib[0, r].astype(jnp.float32)
        second = ib[1, r].astype(jnp.float32)
        merged = second + share * (first - second)
        o_ref[0, :, pl.ds((peers + r) * HD, HD)] = merged.astype(jnp.bfloat16)
    await_bytes(o_ref.at[0, :, pl.ds(0, peers * HD)], out_recv.at[0])

    for t in range(3):
        await_bytes(wholes[t].at[pl.ds(0, (peers - 1) * rows)], in_send.at[0, t])
        others = (peers if t == 0 else owners) - 1
        await_bytes(shared[t].at[pl.ds(0, others * rows)], in_send.at[1, t])
    await_bytes(of.at[pl.ds(0, (peers - 1) * rows)], out_send.at[0])
    await_bytes(os.at[pl.ds(0, (peers - 1) * rows)], out_send.at[1])
    await_bytes(sb.at[pl.ds(0, peers - 1)], out_send.at[2])


def exchanged(query_rows, key_rows, value_rows):
    blocks = lax.axis_size("blk")
    ulys = lax.axis_size("uly")
    rows = query_rows.shape[1]
    owners = blocks // 2 * ulys
    peers = blocks * ulys
    full = pltpu.VMEM((peers * rows, HD), jnp.bfloat16)
    less = pltpu.VMEM((owners * rows, HD), jnp.bfloat16)
    return pl.pallas_call(
        functools.partial(exchange_kernel, blocks, ulys, rows),
        out_shape=pltpu.VMEM(query_rows.shape, jnp.bfloat16),
        in_specs=[pl.BlockSpec(memory_space=pl.ANY)] * 3,
        out_specs=pl.BlockSpec(memory_space=pltpu.VMEM),
        scratch_shapes=[
            full, full, full, full, full, less, less, full,
            pltpu.VMEM((peers, 1, HD), jnp.float32),
            pltpu.VMEM((2, owners, rows, HD), jnp.bfloat16),
            pltpu.VMEM((2, owners, 1, HD), jnp.float32),
            pltpu.SemaphoreType.DMA((2, 3)),
            pltpu.SemaphoreType.DMA((7,)),
            pltpu.SemaphoreType.DMA((3,)),
            pltpu.SemaphoreType.DMA((5,)),
            pltpu.SemaphoreType.REGULAR((blocks,)),
        ],
        compiler_params=pltpu.CompilerParams(collective_id=0, has_side_effects=True),
    )(query_rows, key_rows, value_rows)


def local(query_rows, key_rows, value_rows):
    blocks = lax.axis_size("blk")
    ulys = lax.axis_size("uly")
    rows = query_rows.shape[1]
    heads = query_rows.shape[2] // HD
    peers = blocks * ulys
    even = blocks % 2 == 0 and 2 * heads == 3 * peers
    if even and rows * peers <= 1024 and rows <= HD and rows % 16 == 0:
        return exchanged(query_rows, key_rows, value_rows)
    return gathered(query_rows, key_rows, value_rows)


def solution(mesh):
    spec = P("cfg", ("groups", "blk", "uly"), None)
    return jax.shard_map(
        local, mesh=mesh, in_specs=(spec, spec, spec), out_specs=spec, check_vma=False
    )
```
